32 devices in a mesh: dp: 16 (over z, y, x), tensor: 2 (over core).
Axes of the slice: x: 2, y: 2, z: 4, core: 2. Of those that a mesh axis runs over, the one named last changes fastest.
Arguments:
- current: float32 [32, 4096], P('dp'), may hold values from -6 to 6
- noise_draw: float32 [32, 4096], P('dp'), may hold values from -6 to 6
- labels: bfloat16 [32, 1152], P('dp'), may hold values from -6 to 6
- time_now: float32 [32], P('dp'), may hold values from 0.4 to 1
- step_size: float32 [32], P('dp'), may hold values from 0.005 to 0.02
- accept: int32 [32], P('dp'), may hold values 0 or 1
- patch_weight: bfloat16 [16, 1152], replicated, may hold values from -1.5 to 1.5
- time_in: bfloat16 [256, 1152], replicated, may hold values from -0.375 to 0.375
- time_out: bfloat16 [1152, 1152], replicated, may hold values from -0.1875 to 0.1875
- qkv_weight: bfloat16 [1, 1152, 3, 1152], P(None, None, None, 'tensor'), may hold values from -1 to 1
- out_weight: bfloat16 [1, 1152, 1152], P(None, None, 'tensor'), may hold values from -0.1875 to 0.1875
- ada_weight: bfloat16 [1, 1152, 3456], P(None, 'dp', 'tensor'), may hold values from -0.1875 to 0.1875
- final_ada: bfloat16 [1152, 2304], P('dp', 'tensor'), may hold values from -0.1875 to 0.1875
- final_proj: bfloat16 [1152, 16], replicated, may hold values from -0.1875 to 0.1875
Outputs:
- next_state: float32 [32, 4096], P('dp')
- error_norm: float32 [32], P('dp')
The draws below stay inside these ranges and needn't reach their ends.
All inputs are finite; a program needn't handle non-finite values. No bound on the sum of `accept` on one device may be relied on, other than what follows from the above.
Results may differ from the reference program's by a relative error of at most 0.015.
Values may be sent and summed in bfloat16 or wider, within the bound.
No kernel may reach another device: no remote copies, remote signals or barrier semaphores. Data moves between devices by JAX's collectives and lax.ppermute only.
A program may use at most 128 MiB of HBM per device.

```python
import math
import jax
import jax.numpy as jnp
from jax import lax

D = 1152
HEADS = 16
TOK = 256
FREQ = 256
PATCH_VALS = 16
LAYERS = 1
HEAD_DIM = 72
LATENT = 4096
BATCH = 32
N_TENSOR = 2


def draw_qkv_weight(key, part):
    key_one = jax.random.fold_in(jax.random.fold_in(key, 17), 0)
    spread = D ** (-0.5)
    whole = jax.random.normal(key_one, (LAYERS, D, 3, D), jnp.float32) * spread
    return jnp.clip(whole, -1.0, 1.0).astype(jnp.bfloat16)


def plant(result, rng, low, top_value):
    longest = result.shape.index(max(result.shape))
    spots = []
    for shift in (0, 1):
        where = [jax.random.randint(jax.random.fold_in(rng, axis), (), 0, length) for axis, length in enumerate(result.shape)]
        where[longest] = (where[longest] + shift) % result.shape[longest]
        spots.append(tuple(where))
    return result.at[spots[0]].set(low).at[spots[1]].set(top_value)


def block_levels(stream_key, dims, pieces, low, top_value):
    factor_of, own = 1.0, jax.random.fold_in(stream_key, 6)
    for axis_at, blocks in pieces:
        heights = jnp.exp(jax.random.uniform(jax.random.fold_in(own, axis_at), (blocks,), jnp.float32, low / len(pieces), top_value / len(pieces)))
        factor_of = factor_of * jnp.repeat(heights, dims[axis_at] // blocks).reshape([-1 if axis == axis_at else 1 for axis in range(len(dims))])
    return factor_of


def scatter_about(own_key, extent, scale, bound, shards=(), kind=jnp.bfloat16):
    level = block_levels(own_key, extent, shards, -0.22, 0.18) if shards else 1.0
    result = jax.random.normal(own_key, extent, jnp.float32) * scale * level
    return jnp.minimum(jnp.maximum(result, -bound), bound).astype(kind)


def setup_inputs(seed: int = 0) -> dict:
    seeds = jax.random.split(jax.random.key(seed), 15)
    return {
        "current": scatter_about(seeds[0], (BATCH, LATENT), 1.0, 6.0, ((0, 16),), jnp.float32),
        "noise_draw": scatter_about(seeds[1], (BATCH, LATENT), 1.0, 6.0, ((0, 16),), jnp.float32),
        "labels": scatter_about(seeds[2], (BATCH, D), 1.0, 6.0, ((0, 16),)),
        "time_now": jnp.clip(0.4 + 0.6 * jax.random.uniform(seeds[3], (BATCH,), jnp.float32) ** block_levels(seeds[3], (BATCH,), ((0, 16),), -0.2, 0.2), 0.4, 1.0),
        "step_size": jnp.clip(0.005 + 0.015 * jax.random.uniform(seeds[4], (BATCH,), jnp.float32) ** block_levels(seeds[4], (BATCH,), ((0, 16),), -0.2, 0.2), 0.005, 0.02),
        "accept": plant((jax.random.randint(seeds[5], (BATCH,), 0, 4) < 3).astype(jnp.int32), jax.random.fold_in(seeds[5], 1), 0, 1),
        "patch_weight": scatter_about(seeds[6], (PATCH_VALS, D), PATCH_VALS ** -0.5, 1.5),
        "time_in": scatter_about(seeds[7], (FREQ, D), FREQ ** -0.5, 0.375),
        "time_out": scatter_about(seeds[8], (D, D), D ** -0.5, 0.1875),
        "qkv_weight": draw_qkv_weight(jax.random.fold_in(seeds[14], 71), 0),
        "out_weight": scatter_about(seeds[10], (LAYERS, D, D), D ** -0.5, 0.1875, ((2, 2),)),
        "ada_weight": scatter_about(seeds[11], (LAYERS, D, 3 * D), D ** -0.5, 0.1875, ((1, 16), (2, 2))),
        "final_ada": scatter_about(seeds[12], (D, 2 * D), D ** -0.5, 0.1875, ((0, 16), (1, 2))),
        "final_proj": scatter_about(seeds[13], (D, PATCH_VALS), D ** -0.5, 0.1875),
    }


beta_low = 0.1
beta_high = 20.0
tol_abs = 0.0078
tol_rel = 0.05
norm_eps = 1e-06

def beta_at(moments):
    return beta_low + (beta_high - beta_low) * moments

def sigma_at(moments):
    integral = beta_low * moments + 0.5 * (beta_high - beta_low) * moments * moments
    return jnp.sqrt(1.0 - jnp.exp(-integral))

def time_features(moments, feature_count):
    half_count = feature_count // 2
    freq_index = jnp.arange(half_count, dtype=jnp.float32)
    freq_rates = jnp.exp(-math.log(10000.0) * freq_index / half_count)
    angles = 1000.0 * moments[:, None] * freq_rates[None, :]
    return jnp.concatenate([jnp.cos(angles), jnp.sin(angles)], axis=1)

def position_table(positions, feature_count):
    half_count = feature_count // 2
    freq_index = jnp.arange(half_count, dtype=jnp.float32)
    freq_rates = jnp.exp(-math.log(10000.0) * freq_index / half_count)
    angles = positions.astype(jnp.float32)[:, None] * freq_rates[None, :]
    return jnp.concatenate([jnp.sin(angles), jnp.cos(angles)], axis=1)

def condition(moments, labels, time_in, time_out):
    features = time_features(moments, time_in.shape[0]).astype(jnp.bfloat16)
    hidden = jax.nn.silu(jnp.dot(features, time_in, preferred_element_type=jnp.float32)).astype(jnp.bfloat16)
    joined = labels.astype(jnp.float32) + jnp.dot(hidden, time_out, preferred_element_type=jnp.float32)
    return jax.nn.silu(joined).astype(jnp.bfloat16)

def layer_norm(values):
    average = lax.optimization_barrier(jnp.mean(values, axis=-1, keepdims=True))
    centred = values - average
    spread_sq = lax.optimization_barrier(jnp.mean(centred * centred, axis=-1, keepdims=True))
    return centred * lax.rsqrt(spread_sq + norm_eps)

def modulate(values, shift_vec, scale_vec):
    return (layer_norm(values) * (1.0 + scale_vec) + shift_vec).astype(jnp.bfloat16)

def rounded(values):
    return lax.optimization_barrier(values.astype(jnp.bfloat16)).astype(jnp.float32)

def drift(values, moments, noise_guess):
    beta_rate = beta_at(moments)[:, None]
    return 0.5 * beta_rate * values - beta_rate * noise_guess / sigma_at(moments)[:, None]

def denoise(latents, moments, labels, patch_weight, time_in, time_out, qkv_weight, out_weight, ada_weight, final_ada, final_proj):
    cond_act = condition(moments, labels, time_in, time_out)
    layer_mods = jnp.stack([jnp.dot(cond_act, ada_weight[block_index], preferred_element_type=jnp.float32) for block_index in range(LAYERS)], axis=1)
    final_mods = jnp.dot(cond_act, final_ada, preferred_element_type=jnp.float32)
    positions = position_table(jnp.arange(TOK, dtype=jnp.int32), D)
    groups = N_TENSOR
    highest = lax.Precision.HIGHEST

    def one_latent(inputs):
        latent, mod_rows, final_rows = inputs
        tokens = latent.reshape(TOK, PATCH_VALS).astype(jnp.bfloat16)
        stream = jnp.dot(tokens, patch_weight, preferred_element_type=jnp.float32) + positions
        for block_index in range(LAYERS):
            shift_attn, scale_attn, gate_attn = jnp.split(mod_rows[block_index], 3)
            attn_in = modulate(stream, shift_attn, scale_attn)
            projected = jnp.dot(attn_in, qkv_weight[block_index].reshape(D, 3 * D), preferred_element_type=jnp.float32)
            projected = rounded(projected).reshape(TOK, 3, HEADS, HEAD_DIM)
            scores = jnp.einsum('qhe,khe->hqk', projected[:, 0], projected[:, 1], precision=highest) * HEAD_DIM ** (-0.5)
            attn_probs = rounded(jax.nn.softmax(scores, axis=-1))
            attended = rounded(jnp.einsum('hqk,khe->qhe', attn_probs, projected[:, 2], precision=highest))
            attended = attended.reshape(TOK, groups, D // groups)
            out_groups = out_weight[block_index].reshape(D, groups, D // groups).astype(jnp.float32)
            partial_value = rounded(jnp.einsum('qgk,dgk->gqd', attended, out_groups, precision=highest))
            stream = stream + gate_attn * lax.optimization_barrier(jnp.sum(partial_value, axis=0))
        shift_final, scale_final = jnp.split(final_rows, 2)
        final_in = modulate(stream, shift_final, scale_final)
        return jnp.dot(final_in, final_proj, preferred_element_type=jnp.float32).reshape(LATENT)
    return lax.map(one_latent, (latents, layer_mods, final_mods))

def reference(current, noise_draw, labels, time_now, step_size, accept, patch_weight, time_in, time_out, qkv_weight, out_weight, ada_weight, final_ada, final_proj):
    noise_now = denoise(current, time_now, labels, patch_weight, time_in, time_out, qkv_weight, out_weight, ada_weight, final_ada, final_proj)
    drift_now = drift(current, time_now, noise_now)
    spread = jnp.sqrt(step_size * beta_at(time_now))[:, None] * noise_draw
    euler_state = current + step_size[:, None] * drift_now + spread
    later_time = time_now - step_size
    noise_later = denoise(euler_state, later_time, labels, patch_weight, time_in, time_out, qkv_weight, out_weight, ada_weight, final_ada, final_proj)
    drift_later = drift(euler_state, later_time, noise_later)
    heun_state = current + 0.5 * step_size[:, None] * (drift_now + drift_later) + spread
    scale_ref = jnp.maximum(tol_abs, tol_rel * jnp.maximum(jnp.abs(heun_state), jnp.abs(current)))
    scaled_gap = (euler_state - heun_state) / scale_ref
    error_norm = jnp.sqrt(lax.optimization_barrier(jnp.sum(scaled_gap * scaled_gap, axis=1)) / LATENT)
    next_state = jnp.where(accept[:, None] == 1, heun_state, current)
    return (next_state, error_norm)
```

```python
import functools
import math

import jax
import jax.numpy as jnp
import numpy as np
from jax import lax
from jax.experimental import pallas as pl
from jax.experimental.pallas import tpu as pltpu
from jax.sharding import PartitionSpec as P

HEAD_DIM = 72
LANES = 128
ROWS = 8

beta_low = 0.1
beta_high = 20.0
tol_abs = 0.0078
tol_rel = 0.05
norm_eps = 1e-06

f32 = jnp.float32
bf16 = jnp.bfloat16
VM = pl.BlockSpec(memory_space=pltpu.VMEM)
SM = pl.BlockSpec(memory_space=pltpu.SMEM)


def up(size, unit):
    return -(-size // unit) * unit


def mm(a, b):
    return lax.dot_general(a, b, (((1,), (0,)), ((), ())), preferred_element_type=f32)


def mm_t(a, b):
    return lax.dot_general(a, b, (((1,), (1,)), ((), ())), preferred_element_type=f32)


def silu(v):
    return v / (1.0 + jnp.exp(-v))


def position_table(token_count, width):
    half = width // 2
    rates = np.exp(-math.log(10000.0) * np.arange(half) / half)
    angles = np.arange(token_count)[:, None] * rates[None, :]
    return np.concatenate([np.sin(angles), np.cos(angles)], axis=1).astype(np.float32)


def tell_kernel(core_ref, time_ref, step_ref, labels_ref, out_ref, block):
    mine = core_ref[0]
    tiles = labels_ref.shape[1] // LANES
    both = labels_ref[...].astype(f32)
    row = jnp.where(mine == 0, both[0:1], both[1:2])
    block[...] = jnp.zeros_like(block)
    for tile in range(tiles):
        block[tile : tile + 1, :] = row[:, tile * LANES : (tile + 1) * LANES]
    now = time_ref[mine]
    later = now - step_ref[mine]
    block[tiles : tiles + 1, :] = jnp.full((1, LANES), now, f32)
    block[tiles + 1 : tiles + 2, :] = jnp.full((1, LANES), later, f32)
    for dest in range(out_ref.shape[0]):
        out_ref[dest] = block[...]


def part_kernel(
    place_ref, heard_ref, rates_ref, time_in_ref, time_out_ref,
    ada_own, ada_other, fin_own, fin_other, out_ref, part,
):
    count = heard_ref.shape[0]
    width = time_out_ref.shape[0]
    tiles = width // LANES
    own_rows = ada_own.shape[0]
    labels = jnp.concatenate([heard_ref[:, tile, :] for tile in range(tiles)], axis=1)
    labels = jnp.concatenate([labels, labels], axis=0)
    moments = jnp.concatenate([heard_ref[:, tiles, :], heard_ref[:, tiles + 1, :]], axis=0)
    angles = 1000.0 * moments * rates_ref[...]
    features = jnp.concatenate([jnp.cos(angles), jnp.sin(angles)], axis=1).astype(bf16)
    hidden = silu(mm(features, time_in_ref[...])).astype(bf16)
    cond = silu(labels + mm(hidden, time_out_ref[...])).astype(bf16)
    first = place_ref[1] * own_rows
    pick_shape = (width, LANES)
    pick = lax.broadcasted_iota(jnp.int32, pick_shape, 0) == (
        lax.broadcasted_iota(jnp.int32, pick_shape, 1) + first
    )
    own_cond = mm(cond, pick.astype(f32).astype(bf16))[:, :own_rows].astype(bf16)
    low = place_ref[0] == 0
    wide = up(ada_own.shape[1], LANES)
    for at, own, other in ((0, ada_own, ada_other), (2 * wide, fin_own, fin_other)):
        a = mm(own_cond, own[...])
        b = mm(own_cond, other[...])
        used = a.shape[1]
        gap = up(used, LANES)
        part[:, at : at + used] = jnp.where(low, a, b)
        part[:, at + gap : at + gap + used] = jnp.where(low, b, a)
        if gap != used:
            part[:, at + used : at + gap] = jnp.zeros((2 * count, gap - used), f32)
            part[:, at + gap + used : at + 2 * gap] = jnp.zeros((2 * count, gap - used), f32)
    for dest in range(count):
        now_row = part[dest : dest + 1, :]
        later_row = part[count + dest : count + dest + 1, :]
        out_ref[dest] = jnp.concatenate([now_row, later_row], axis=0).astype(bf16)


def norm(v):
    width = v.shape[1]
    average = jnp.sum(v, axis=1, keepdims=True) * (1.0 / width)
    centred = v - average
    spread_sq = jnp.sum(centred * centred, axis=1, keepdims=True) * (1.0 / width)
    return centred * lax.rsqrt(spread_sq + norm_eps)


def step_kernel(
    core_ref, time_ref, step_ref, accept_ref, cur_ref, noise_ref, pos_ref, patch_ref,
    qkv_own, qkv_other, out_own, out_other, proj_ref, mods_ref, out_ref,
    cur32, nse32, state32, guess32, modv, patch8, proj8, stream, inner, qkv, mixed,
):
    mine = core_ref[0]
    low_core = mine == 0
    lat_rows = cur32.shape[0]
    tokens, width = stream.shape
    half = qkv_own.shape[2]
    padded = qkv.shape[3]
    heads = half // HEAD_DIM
    count = mods_ref.shape[0]
    vals = patch_ref.shape[0]
    reps = LANES // vals

    for row in range(lat_rows):
        lanes = slice(row * LANES, (row + 1) * LANES)
        cur32[row : row + 1, :] = jnp.where(low_core, cur_ref[0:1, lanes], cur_ref[1:2, lanes])
        nse32[row : row + 1, :] = jnp.where(low_core, noise_ref[0:1, lanes], noise_ref[1:2, lanes])
    for rep in range(reps):
        patch8[rep * vals : (rep + 1) * vals, :] = patch_ref[...]
        proj8[rep * vals : (rep + 1) * vals, :] = proj_ref[...]
    if padded != half:
        qkv[:, :, :, half:] = jnp.zeros(qkv.shape[:3] + (padded - half,), bf16)

    total = mods_ref[0].astype(f32)
    for source in range(1, count):
        total = total + mods_ref[source].astype(f32)
    lay_cols = 3 * width // 2
    wide = up(lay_cols, LANES)
    low = total[:, :wide]
    high = total[:, wide : 2 * wide]
    lane = lax.broadcasted_iota(jnp.int32, (2, width), 1)
    rest = low[:, width:]
    rest = jnp.concatenate([rest, jnp.zeros((2, width - rest.shape[1]), f32)], axis=1)
    split = lay_cols - width
    scale_attn = jnp.where(lane < split, rest, pltpu.roll(high[:, :width], split, 1))
    gate_attn = pltpu.roll(high, wide - (width - split), 1)[:, :width]
    for moment in range(2):
        row = slice(moment, moment + 1)
        modv[moment, 0:1, :] = low[row, :width]
        modv[moment, 1:2, :] = 1.0 + scale_attn[row]
        modv[moment, 2:3, :] = gate_attn[row]
        modv[moment, 3:4, :] = total[row, 2 * wide : 2 * wide + width]
        modv[moment, 4:5, :] = 1.0 + total[row, 2 * wide + width : 2 * wide + 2 * width]

    now = jnp.full((1, LANES), time_ref[mine], f32)
    step = jnp.full((1, LANES), step_ref[mine], f32)
    later = now - step

    def beta_at(m):
        return beta_low + (beta_high - beta_low) * m

    def drift(values, m, guess):
        rate = beta_at(m)
        integral = beta_low * m + 0.5 * (beta_high - beta_low) * m * m
        return 0.5 * rate * values - rate * guess / jnp.sqrt(1.0 - jnp.exp(-integral))

    spread = jnp.sqrt(step * beta_at(now)) * nse32[...]
    group = lax.broadcasted_iota(jnp.int32, (tokens, LANES), 1) // vals
    own_slot = group == lax.broadcasted_iota(jnp.int32, (tokens, LANES), 0) % reps
    exp_scale = HEAD_DIM**-0.5 * math.log2(math.e)

    def evaluate(index, carry):
        del carry
        x = state32[...]
        tok = jnp.broadcast_to(x[:, None, :], (lat_rows, reps, LANES)).reshape(tokens, LANES)
        tok = jnp.where(own_slot, tok, 0.0).astype(bf16)
        stream[...] = mm(tok, patch8[...]) + pos_ref[...]
        inner[...] = (norm(stream[...]) * modv[index, 1:2, :] + modv[index, 0:1, :]).astype(bf16)
        for part, weight in enumerate((qkv_own, qkv_other)):
            for kind in range(3):
                qkv[part, kind, :, :half] = mm(inner[...], weight[kind]).astype(bf16)
        for part in range(2):
            mixed[...] = jnp.zeros_like(mixed)
            for head in range(heads):
                begin = head * HEAD_DIM
                lo = begin // LANES * LANES
                hi = up(begin + HEAD_DIM, LANES)
                at = lax.broadcasted_iota(jnp.int32, (tokens, hi - lo), 1) + lo
                inside = (at >= begin) & (at < begin + HEAD_DIM)
                q = jnp.where(inside, qkv[part, 0, :, lo:hi], jnp.zeros((), bf16))
                v = jnp.where(inside, qkv[part, 2, :, lo:hi], jnp.zeros((), bf16))
                scores = mm_t(q, qkv[part, 1, :, lo:hi])
                top = jnp.max(scores, axis=1, keepdims=True)
                probs = jnp.exp2((scores - top) * exp_scale)
                scale = 1.0 / jnp.sum(probs, axis=1, keepdims=True)
                mixed[:, lo:hi] += mm(probs.astype(bf16), v) * scale
            weight = (out_own, out_other)[part]
            value = mm(mixed[:, :half].astype(bf16), weight[...])
            stream[...] += modv[index, 2:3, :] * value
        inner[...] = (norm(stream[...]) * modv[index, 4:5, :] + modv[index, 3:4, :]).astype(bf16)
        guess = jnp.where(own_slot, mm_t(inner[...], proj8[...]), 0.0)
        guess = jnp.sum(guess.reshape(lat_rows, reps, LANES), axis=1)
        guess32[index] = guess

        @pl.when(index == 0)
        def _():
            state32[...] = cur32[...] + step * drift(cur32[...], now, guess) + spread

        return 0

    state32[...] = cur32[...]
    lax.fori_loop(0, 2, evaluate, 0)

    cur = cur32[...]
    euler = state32[...]
    drift_now = drift(cur, now, guess32[0])
    drift_later = drift(euler, later, guess32[1])
    heun = cur + 0.5 * step * (drift_now + drift_later) + spread
    scale_ref = jnp.maximum(tol_abs, tol_rel * jnp.maximum(jnp.abs(heun), jnp.abs(cur)))
    gap = (euler - heun) / scale_ref
    square = jnp.sum(jnp.sum(gap * gap, axis=1, keepdims=True), axis=0, keepdims=True)
    error = jnp.sqrt(square / (lat_rows * LANES))
    out_ref[:lat_rows, :] = jnp.where(accept_ref[mine] == 1, heun, cur)
    out_ref[lat_rows:, :] = jnp.broadcast_to(error, (ROWS, LANES))


def shards(
    current, noise_draw, labels, time_now, step_size, accept, patch_weight, time_in,
    time_out, qkv_weight, out_weight, ada_weight, final_ada, final_proj,
):
    count = lax.axis_size("dp")
    width = time_out.shape[0]
    latent = current.shape[1]
    vals = patch_weight.shape[0]
    tokens = latent // vals
    half = qkv_weight.shape[3]
    core = lax.axis_index("tensor").astype(jnp.int32)
    place = jnp.stack([core, lax.axis_index("dp").astype(jnp.int32)])
    swap = functools.partial(lax.ppermute, axis_name="tensor", perm=[(0, 1), (1, 0)])

    qkv = qkv_weight[0].transpose(1, 0, 2)
    out = out_weight[0].T
    ada = ada_weight[0]

    ada_other, fin_other = swap(ada), swap(final_ada)
    qkv_other, out_other = swap(qkv), swap(out)

    tell_rows = up(width // LANES + 2, ROWS)
    told = pl.pallas_call(
        tell_kernel,
        out_shape=jax.ShapeDtypeStruct((count, tell_rows, LANES), f32),
        in_specs=[SM, SM, SM, VM],
        out_specs=VM,
        scratch_shapes=[pltpu.VMEM((tell_rows, LANES), f32)],
        compiler_params=pltpu.CompilerParams(vmem_limit_bytes=4 << 20),
    )(place, time_now, step_size, labels)
    heard = lax.all_to_all(told, "dp", 0, 0, tiled=True)

    half_freq = time_in.shape[0] // 2
    rates = np.exp(-math.log(10000.0) * np.arange(half_freq) / half_freq)
    rates = jnp.asarray(rates.astype(np.float32)[None])
    cols = 2 * up(ada.shape[1], LANES) + 2 * final_ada.shape[1]
    parts = pl.pallas_call(
        part_kernel,
        out_shape=jax.ShapeDtypeStruct((count, 2, cols), bf16),
        in_specs=[SM] + [VM] * 8,
        out_specs=VM,
        scratch_shapes=[pltpu.VMEM((2 * count, cols), f32)],
        compiler_params=pltpu.CompilerParams(vmem_limit_bytes=16 << 20),
    )(place, heard, rates, time_in, time_out, ada, ada_other, final_ada, fin_other)
    mods = lax.all_to_all(parts, "dp", 0, 0, tiled=True)

    lat_rows = latent // LANES
    padded = up(half, LANES)
    positions = jnp.asarray(position_table(tokens, width))
    small = pltpu.VMEM((lat_rows, LANES), f32)
    done = pl.pallas_call(
        step_kernel,
        out_shape=jax.ShapeDtypeStruct((lat_rows + ROWS, LANES), f32),
        in_specs=[SM] * 4 + [VM] * 10,
        out_specs=VM,
        scratch_shapes=[
            small, small, small,
            pltpu.VMEM((2, lat_rows, LANES), f32),
            pltpu.VMEM((2, ROWS, width), f32),
            pltpu.VMEM((LANES, width), bf16),
            pltpu.VMEM((LANES, width), bf16),
            pltpu.VMEM((tokens, width), f32),
            pltpu.VMEM((tokens, width), bf16),
            pltpu.VMEM((2, 3, tokens, padded), bf16),
            pltpu.VMEM((tokens, padded), f32),
        ],
        compiler_params=pltpu.CompilerParams(vmem_limit_bytes=40 << 20),
    )(
        place, time_now, step_size, accept, current, noise_draw, positions, patch_weight,
        qkv, qkv_other, out, out_other, final_proj.T, mods,
    )
    other = swap(done)
    first = jnp.where(core == 0, done, other)
    second = jnp.where(core == 0, other, done)
    both = jnp.stack([first, second])
    next_state = both[:, :lat_rows].reshape(2, latent)
    return (next_state, both[:, lat_rows, 0])


def solution(mesh):
    in_specs = (
        P("dp", None),
        P("dp", None),
        P("dp", None),
        P("dp"),
        P("dp"),
        P("dp"),
        P(),
        P(),
        P(),
        P(None, None, None, "tensor"),
        P(None, None, "tensor"),
        P(None, "dp", "tensor"),
        P("dp", "tensor"),
        P(),
    )
    out_specs = (P("dp", None), P("dp"))
    return jax.shard_map(shards, mesh=mesh, in_specs=in_specs, out_specs=out_specs, check_vma=False)
```

```python
import functools
import math

import jax
import jax.numpy as jnp
import numpy as np
from jax import lax
from jax.experimental import pallas as pl
from jax.experimental.pallas import tpu as pltpu
from jax.sharding import PartitionSpec as P

HEAD_DIM = 72
LANES = 128
ROWS = 8
SUB = 16
AHEAD = 2
SLOTS = 4
GRANT = 60 << 20

beta_low = 0.1
beta_high = 20.0
tol_abs = 0.0078
tol_rel = 0.05
norm_eps = 1e-06

f32 = jnp.float32
bf16 = jnp.bfloat16
VM = pl.BlockSpec(memory_space=pltpu.VMEM)
HBM = pl.BlockSpec(memory_space=pltpu.HBM)
SM = pl.BlockSpec(memory_space=pltpu.SMEM)


def up(size, unit):
    return -(-size // unit) * unit


def mm(a, b):
    return lax.dot_general(a, b, (((1,), (0,)), ((), ())), preferred_element_type=f32)


def mm_t(a, b):
    return lax.dot_general(a, b, (((1,), (1,)), ((), ())), preferred_element_type=f32)


def start_copies(sources, targets, sems):
    copies = [
        pltpu.make_async_copy(source, target, sems.at[i])
        for i, (source, target) in enumerate(zip(sources, targets))
    ]
    for copy in copies:
        copy.start()
    return copies


def like(arrays):
    return [pltpu.VMEM(a.shape, a.dtype) for a in arrays]


def silu(v):
    return v / (1.0 + jnp.exp(-v))


def position_table(token_count, width):
    half = width // 2
    rates = np.exp(-math.log(10000.0) * np.arange(half) / half)
    angles = np.arange(token_count)[:, None] * rates[None, :]
    return np.concatenate([np.sin(angles), np.cos(angles)], axis=1).astype(np.float32)


def tell_kernel(time_hbm, step_hbm, labels_hbm, out_ref, time_ref, step_ref, labels_ref, block, sems):
    copies = start_copies(
        (time_hbm, step_hbm, labels_hbm), (time_ref, step_ref, labels_ref), sems
    )
    block[...] = jnp.zeros_like(block)
    for copy in copies:
        copy.wait()
    mine = lax.axis_index("tensor")
    tiles = labels_ref.shape[1] // LANES
    both = labels_ref[...].astype(f32)
    row = jnp.where(mine == 0, both[0:1], both[1:2])
    for tile in range(tiles):
        block[tile : tile + 1, :] = row[:, tile * LANES : (tile + 1) * LANES]
    now = time_ref[mine]
    later = now - step_ref[mine]
    block[tiles : tiles + 1, :] = jnp.full((1, LANES), now, f32)
    block[tiles + 1 : tiles + 2, :] = jnp.full((1, LANES), later, f32)
    for dest in range(out_ref.shape[0]):
        out_ref[dest] = block[...]


def part_kernel(heard_ref, *refs):
    sources, out_ref, sems = refs[:10], refs[10], refs[-1]
    time_in_ref, time_out_ref, ada_near, ada_far, fin_near, fin_far, part = refs[11:18]
    own_rows = sources[2].shape[0]
    second = up(own_rows, SUB)
    stacks = (ada_near, ada_far, fin_near, fin_far)
    stages = refs[18:-1]
    copies = [
        pltpu.make_async_copy(sources[0], time_in_ref, sems.at[0]),
        pltpu.make_async_copy(sources[1], time_out_ref, sems.at[1]),
    ]
    for at, source in enumerate(sources[2:]):
        stack = stacks[at // 2]
        first = at % 2 * second
        target = stages[at] if stages else stack.at[pl.ds(first, own_rows), :]
        copies.append(pltpu.make_async_copy(source, target, sems.at[2 + at]))
    for copy in copies:
        copy.start()
    count = heard_ref.shape[0]
    width = time_out_ref.shape[0]
    tiles = width // LANES
    labels = jnp.concatenate([heard_ref[:, tile, :] for tile in range(tiles)], axis=1)
    labels = jnp.concatenate([labels, labels], axis=0)
    moments = jnp.concatenate([heard_ref[:, tiles, :], heard_ref[:, tiles + 1, :]], axis=0)
    half_freq = time_in_ref.shape[0] // 2
    index = lax.broadcasted_iota(jnp.int32, (1, half_freq), 1).astype(f32)
    rates = jnp.exp(index * (-math.log(10000.0) / half_freq))
    angles = 1000.0 * moments * rates
    features = jnp.concatenate([jnp.cos(angles), jnp.sin(angles)], axis=1).astype(bf16)
    place = lax.axis_index("dp")
    pair = place + 1 - 2 * lax.rem(place, 2)
    depth = ada_near.shape[0]
    pick_shape = (width, depth)
    at_row = lax.broadcasted_iota(jnp.int32, pick_shape, 0)
    at_lane = lax.broadcasted_iota(jnp.int32, pick_shape, 1)
    mine = (at_lane < own_rows) & (at_row == at_lane + place * own_rows)
    theirs = (at_lane >= second) & (at_lane < second + own_rows)
    theirs = theirs & (at_row == at_lane - second + pair * own_rows)
    pick = jnp.where(mine | theirs, 1.0, 0.0).astype(bf16)
    copies[0].wait()
    hidden = silu(mm(features, time_in_ref[...])).astype(bf16)
    copies[1].wait()
    cond = silu(labels + mm(hidden, time_out_ref[...])).astype(bf16)
    own_cond = mm(cond, pick).astype(bf16)
    low = lax.axis_index("tensor") == 0
    for copy in copies[2:]:
        copy.wait()
    for at, stage in enumerate(stages):
        first = at % 2 * second
        stacks[at // 2][first : first + own_rows, :] = stage[...]
    if second != own_rows:
        for stack in stacks:
            for first in (own_rows, second + own_rows):
                stack[first : first + second - own_rows, :] = jnp.zeros(
                    (second - own_rows, stack.shape[1]), bf16
                )
    wide = up(ada_near.shape[1], LANES)
    for at, near, far in ((0, ada_near, ada_far), (2 * wide, fin_near, fin_far)):
        a = mm(own_cond, near[...])
        b = mm(own_cond, far[...])
        used = a.shape[1]
        gap = up(used, LANES)
        part[:, at : at + used] = jnp.where(low, a, b)
        part[:, at + gap : at + gap + used] = jnp.where(low, b, a)
        if gap != used:
            part[:, at + used : at + gap] = jnp.zeros((2 * count, gap - used), f32)
            part[:, at + gap + used : at + 2 * gap] = jnp.zeros((2 * count, gap - used), f32)
    for dest in range(count):
        now_row = part[dest : dest + 1, :]
        later_row = part[count + dest : count + dest + 1, :]
        out_ref[dest] = jnp.concatenate([now_row, later_row], axis=0).astype(bf16)


def norm(v):
    width = v.shape[1]
    average = jnp.sum(v, axis=1, keepdims=True) * (1.0 / width)
    centred = v - average
    spread_sq = jnp.sum(centred * centred, axis=1, keepdims=True) * (1.0 / width)
    return centred * lax.rsqrt(spread_sq + norm_eps)


def step_kernel(
    time_hbm, step_hbm, accept_hbm, mods_ref, *refs,
):
    sources, out_ref, rest_refs = refs[:9], refs[9], refs[18:]
    cur_ref, noise_ref, patch_ref, pos_ref, qkv_own, qkv_other, out_all, proj_ref = refs[10:18]
    half = qkv_own.shape[1]
    targets = (
        cur_ref, noise_ref, patch_ref, pos_ref, qkv_own, qkv_other,
        out_all.at[pl.ds(0, half), :], out_all.at[pl.ds(half, half), :], proj_ref,
    )
    time_ref, step_ref, accept_ref, sems, *work = rest_refs
    early = start_copies(
        (time_hbm, step_hbm, accept_hbm), (time_ref, step_ref, accept_ref), sems.at[pl.ds(9, 3)]
    )
    copies = [pltpu.make_async_copy(s, t, sems.at[i]) for i, (s, t) in enumerate(zip(sources, targets))]
    for at in (0, 1, 2, 8, 3, 4, 5, 6, 7):
        copies[at].start()
    for copy in early + copies[:3] + copies[8:]:
        copy.wait()
    step_body(
        time_ref, step_ref, accept_ref, cur_ref, noise_ref, pos_ref, patch_ref,
        qkv_own, qkv_other, out_all, proj_ref, mods_ref, out_ref, copies[3:8], *work,
    )


def step_body(
    time_ref, step_ref, accept_ref, cur_ref, noise_ref, pos_ref, patch_ref,
    qkv_own, qkv_other, out_all, proj_ref, mods_ref, out_ref, copies,
    cur32, nse32, state32, guess32, modv, patch8, proj8, stream, inner, query, keys, value, mixed,
    scores, probs, turned,
):
    mine = lax.axis_index("tensor")
    low_core = mine == 0
    lat_rows = cur32.shape[0]
    tokens, width = stream.shape
    half = qkv_own.shape[1]
    heads = half // HEAD_DIM
    count = mods_ref.shape[0]
    vals = patch_ref.shape[0]
    reps = LANES // vals

    for row in range(lat_rows):
        lanes = slice(row * LANES, (row + 1) * LANES)
        cur32[row : row + 1, :] = jnp.where(low_core, cur_ref[0:1, lanes], cur_ref[1:2, lanes])
        nse32[row : row + 1, :] = jnp.where(low_core, noise_ref[0:1, lanes], noise_ref[1:2, lanes])
    for rep in range(reps):
        patch8[rep * vals : (rep + 1) * vals, :] = patch_ref[...]
        proj8[rep * vals : (rep + 1) * vals, :] = proj_ref[...]
    query[:, half:, :] = jnp.zeros((2, query.shape[1] - half, tokens), bf16)
    keys[:, :, half:] = jnp.zeros((2, tokens, keys.shape[2] - half), bf16)

    total = mods_ref[0].astype(f32)
    for source in range(1, count):
        total = total + mods_ref[source].astype(f32)
    lay_cols = 3 * width // 2
    wide = up(lay_cols, LANES)
    low = total[:, :wide]
    high = total[:, wide : 2 * wide]
    lane = lax.broadcasted_iota(jnp.int32, (2, width), 1)
    rest = low[:, width:]
    rest = jnp.concatenate([rest, jnp.zeros((2, width - rest.shape[1]), f32)], axis=1)
    split = lay_cols - width
    scale_attn = jnp.where(lane < split, rest, pltpu.roll(high[:, :width], split, 1))
    gate_attn = pltpu.roll(high, wide - (width - split), 1)[:, :width]
    for moment in range(2):
        row = slice(moment, moment + 1)
        modv[moment, 0:1, :] = low[row, :width]
        modv[moment, 1:2, :] = 1.0 + scale_attn[row]
        modv[moment, 2:3, :] = gate_attn[row]
        modv[moment, 3:4, :] = total[row, 2 * wide : 2 * wide + width]
        modv[moment, 4:5, :] = 1.0 + total[row, 2 * wide + width : 2 * wide + 2 * width]

    now = jnp.full((1, LANES), time_ref[mine], f32)
    step = jnp.full((1, LANES), step_ref[mine], f32)
    later = now - step

    def beta_at(m):
        return beta_low + (beta_high - beta_low) * m

    def drift(values, m, guess):
        rate = beta_at(m)
        integral = beta_low * m + 0.5 * (beta_high - beta_low) * m * m
        return 0.5 * rate * values - rate * guess / jnp.sqrt(1.0 - jnp.exp(-integral))

    spread = jnp.sqrt(step * beta_at(now)) * nse32[...]
    group = lax.broadcasted_iota(jnp.int32, (tokens, LANES), 1) // vals
    own_slot = group == lax.broadcasted_iota(jnp.int32, (tokens, LANES), 0) % reps
    exp_scale = HEAD_DIM**-0.5 * math.log2(math.e)

    def fetched(index, which):
        @pl.when(index == 0)
        def _():
            copies[which].wait()

    ones = jnp.ones((ROWS, tokens), f32)

    def project(part, kind, weight):
        raw = mm_t(weight[kind], inner[...])
        if kind == 0:
            query[part, :half, :] = raw.astype(bf16)
        elif kind == 1:
            keys[part, :, :half] = raw.astype(bf16).T
        else:
            for head in range(heads):
                rows = slice(head * HEAD_DIM, (head + 1) * HEAD_DIM)
                value[part, head] = jnp.concatenate([raw[rows], ones], axis=0).astype(bf16)

    def score(at):
        part, head = divmod(at, heads)
        begin = head * HEAD_DIM
        lo = begin // LANES * LANES
        hi = up(begin + HEAD_DIM, LANES)
        row = lax.broadcasted_iota(jnp.int32, (hi - lo, tokens), 0) + lo
        inside = (row >= begin) & (row < begin + HEAD_DIM)
        q = jnp.where(inside, query[part, lo:hi, :], jnp.zeros((), bf16))
        scores[at % SLOTS] = mm(keys[part, :, lo:hi], q)

    def evaluate(index, carry):
        del carry
        x = state32[...]
        tok = jnp.broadcast_to(x[:, None, :], (lat_rows, reps, LANES)).reshape(tokens, LANES)
        tok = jnp.where(own_slot, tok, 0.0).astype(bf16)
        fetched(index, 0)
        stream[...] = mm(tok, patch8[...]) + pos_ref[...]
        inner[...] = (norm(stream[...]) * modv[index, 1:2, :] + modv[index, 0:1, :]).astype(bf16)
        fetched(index, 1)
        for kind in range(3):
            project(0, kind, qkv_own)
        fetched(index, 2)
        for at in range(AHEAD):
            score(at)
        got = {}
        for at in range(2 * heads):
            if at < 3:
                project(1, (1, 0, 2)[at], qkv_other)
            raw = scores[at % SLOTS]
            top = jnp.max(raw, axis=0, keepdims=True)
            probs[at % 2] = jnp.exp2((raw - top) * exp_scale).astype(bf16)
            if at + AHEAD < 2 * heads:
                score(at + AHEAD)
            part, head = divmod(at, heads)
            mix = mm(value[part, head], probs[at % 2])
            got[at] = mix[:HEAD_DIM] * (1.0 / mix[HEAD_DIM : HEAD_DIM + 1])
            if at % 2:
                pair = jnp.concatenate([got.pop(at - 1), got.pop(at)], axis=0)
                first = (at - 1) * HEAD_DIM
                mixed[first : first + 2 * HEAD_DIM, :] = pair.astype(bf16)
        fetched(index, 3)
        fetched(index, 4)
        turned[...] = mixed[...].T
        stream[...] += modv[index, 2:3, :] * mm(turned[...], out_all[...])
        inner[...] = (norm(stream[...]) * modv[index, 4:5, :] + modv[index, 3:4, :]).astype(bf16)
        guess = jnp.where(own_slot, mm_t(inner[...], proj8[...]), 0.0)
        guess = jnp.sum(guess.reshape(lat_rows, reps, LANES), axis=1)
        guess32[index] = guess

        @pl.when(index == 0)
        def _():
            state32[...] = cur32[...] + step * drift(cur32[...], now, guess) + spread

        return 0

    state32[...] = cur32[...]
    lax.fori_loop(0, 2, evaluate, 0)

    cur = cur32[...]
    euler = state32[...]
    drift_now = drift(cur, now, guess32[0])
    drift_later = drift(euler, later, guess32[1])
    heun = cur + 0.5 * step * (drift_now + drift_later) + spread
    scale_ref = jnp.maximum(tol_abs, tol_rel * jnp.maximum(jnp.abs(heun), jnp.abs(cur)))
    gap = (euler - heun) / scale_ref
    square = jnp.sum(jnp.sum(gap * gap, axis=1, keepdims=True), axis=0, keepdims=True)
    error = jnp.sqrt(square / (lat_rows * LANES))
    out_ref[:lat_rows, :] = jnp.where(accept_ref[mine] == 1, heun, cur)
    out_ref[lat_rows:, :] = jnp.broadcast_to(error, (ROWS, LANES))


def join_kernel(done_ref, other_ref, state_ref, error_ref):
    low = lax.axis_index("tensor") == 0
    lat_rows = state_ref.shape[1] // LANES
    done, other = done_ref[...], other_ref[...]
    first, second = jnp.where(low, done, other), jnp.where(low, other, done)
    for row in range(lat_rows):
        lanes = slice(row * LANES, (row + 1) * LANES)
        state_ref[0:1, lanes] = first[row : row + 1]
        state_ref[1:2, lanes] = second[row : row + 1]
    error_ref[0] = jnp.max(first[lat_rows:])
    error_ref[1] = jnp.max(second[lat_rows:])


def shards(
    current, noise_draw, labels, time_now, step_size, accept, patch_weight, time_in,
    time_out, qkv_weight, out_weight, ada_weight, final_ada, final_proj,
):
    members = lax.axis_size("dp")
    count = members // 2
    groups = [[2 * i + side for i in range(count)] for side in range(2)]
    trade = functools.partial(
        lax.ppermute, axis_name="dp", perm=[(i, i ^ 1) for i in range(members)]
    )
    width = time_out.shape[0]
    latent = current.shape[1]
    vals = patch_weight.shape[0]
    tokens = latent // vals
    half = qkv_weight.shape[3]
    swap = functools.partial(lax.ppermute, axis_name="tensor", perm=[(0, 1), (1, 0)])

    qkv = qkv_weight[0].transpose(1, 2, 0)
    out = out_weight[0].T
    ada = ada_weight[0]

    ada_pair, fin_pair = trade(ada), trade(final_ada)
    ada_other, fin_other = swap(ada), swap(final_ada)
    qkv_other, out_other = swap(qkv), swap(out)

    tell_rows = up(width // LANES + 2, ROWS)
    told = pl.pallas_call(
        tell_kernel,
        out_shape=jax.ShapeDtypeStruct((count, tell_rows, LANES), f32),
        in_specs=[HBM, HBM, HBM],
        out_specs=VM,
        scratch_shapes=[
            pltpu.SMEM(time_now.shape, f32),
            pltpu.SMEM(step_size.shape, f32),
            pltpu.VMEM(labels.shape, labels.dtype),
            pltpu.VMEM((tell_rows, LANES), f32),
            pltpu.SemaphoreType.DMA((3,)),
        ],
        compiler_params=pltpu.CompilerParams(vmem_limit_bytes=GRANT),
    )(time_now, step_size, labels)
    heard = lax.all_to_all(told, "dp", 0, 0, axis_index_groups=groups, tiled=True)
    heard, ada_pair, fin_pair = lax.optimization_barrier((heard, ada_pair, fin_pair))
    ada_pair_other, fin_pair_other = swap(ada_pair), swap(fin_pair)

    cols = 2 * up(ada.shape[1], LANES) + 2 * final_ada.shape[1]
    depth = 2 * up(ada.shape[0], SUB)
    near = (
        time_in, time_out, ada, ada_pair, ada_other, ada_pair_other,
        final_ada, fin_pair, fin_other, fin_pair_other,
    )
    parts = pl.pallas_call(
        part_kernel,
        out_shape=jax.ShapeDtypeStruct((count, 2, cols), bf16),
        in_specs=[VM] + [HBM] * len(near),
        out_specs=VM,
        scratch_shapes=like(near[:2])
        + [pltpu.VMEM((depth, a.shape[1]), bf16) for a in (ada, ada, final_ada, final_ada)]
        + [pltpu.VMEM((2 * count, cols), f32)]
        + (like(near[2:]) if ada.shape[0] % ROWS else [])
        + [pltpu.SemaphoreType.DMA((len(near),))],
        compiler_params=pltpu.CompilerParams(vmem_limit_bytes=GRANT),
    )(heard, *near)
    mods = lax.all_to_all(parts, "dp", 0, 0, axis_index_groups=groups, tiled=True)

    lat_rows = latent // LANES
    padded = up(half, LANES)
    positions = jnp.asarray(position_table(tokens, width))
    small = pltpu.VMEM((lat_rows, LANES), f32)
    held = (
        current, noise_draw, patch_weight, positions, qkv, qkv_other, out, out_other, final_proj.T
    )
    done = pl.pallas_call(
        step_kernel,
        out_shape=jax.ShapeDtypeStruct((lat_rows + ROWS, LANES), f32),
        in_specs=[HBM, HBM, HBM, VM] + [HBM] * len(held),
        out_specs=VM,
        scratch_shapes=like(held[:6])
        + [pltpu.VMEM((width, width), bf16)]
        + like(held[8:])
        + [
            pltpu.SMEM(time_now.shape, f32),
            pltpu.SMEM(step_size.shape, f32),
            pltpu.SMEM(accept.shape, accept.dtype),
            pltpu.SemaphoreType.DMA((len(held) + 3,)),
            small, small, small,
            pltpu.VMEM((2, lat_rows, LANES), f32),
            pltpu.VMEM((2, ROWS, width), f32),
            pltpu.VMEM((LANES, width), bf16),
            pltpu.VMEM((LANES, width), bf16),
            pltpu.VMEM((tokens, width), f32),
            pltpu.VMEM((tokens, width), bf16),
            pltpu.VMEM((2, padded, tokens), bf16),
            pltpu.VMEM((2, tokens, padded), bf16),
            pltpu.VMEM((2, half // HEAD_DIM, HEAD_DIM + ROWS, tokens), bf16),
            pltpu.VMEM((2 * half, tokens), bf16),
            pltpu.VMEM((SLOTS, tokens, tokens), f32),
            pltpu.VMEM((2, tokens, tokens), bf16),
            pltpu.VMEM((tokens, 2 * half), bf16),
        ],
        compiler_params=pltpu.CompilerParams(vmem_limit_bytes=GRANT),
    )(
        time_now, step_size, accept, mods, *held,
    )
    other = swap(done)
    return pl.pallas_call(
        join_kernel,
        out_shape=(
            jax.ShapeDtypeStruct((2, latent), f32),
            jax.ShapeDtypeStruct((2,), f32),
        ),
        in_specs=[VM, VM],
        out_specs=(VM, SM),
    )(done, other)


def solution(mesh):
    in_specs = (
        P("dp", None),
        P("dp", None),
        P("dp", None),
        P("dp"),
        P("dp"),
        P("dp"),
        P(),
        P(),
        P(),
        P(None, None, None, "tensor"),
        P(None, None, "tensor"),
        P(None, "dp", "tensor"),
        P("dp", "tensor"),
        P(),
    )
    out_specs = (P("dp", None), P("dp"))
    return jax.shard_map(shards, mesh=mesh, in_specs=in_specs, out_specs=out_specs, check_vma=False)
```

```python
import functools
import math

import jax
import jax.numpy as jnp
import numpy as np
from jax import lax
from jax.experimental import pallas as pl
from jax.experimental.pallas import tpu as pltpu
from jax.sharding import PartitionSpec as P

HEAD_DIM = 72
LANES = 128
ROWS = 8
SUB = 16
AHEAD = 3
SLOTS = 4
GRANT = 60 << 20
GRANT_ALL = 66_400_000

beta_low = 0.1
beta_high = 20.0
tol_abs = 0.0078
tol_rel = 0.05
norm_eps = 1e-06

f32 = jnp.float32
bf16 = jnp.bfloat16
VM = pl.BlockSpec(memory_space=pltpu.VMEM)
HBM = pl.BlockSpec(memory_space=pltpu.HBM)
SM = pl.BlockSpec(memory_space=pltpu.SMEM)


def up(size, unit):
    return -(-size // unit) * unit


def mm(a, b):
    return lax.dot_general(a, b, (((1,), (0,)), ((), ())), preferred_element_type=f32)


def mm_t(a, b):
    return lax.dot_general(a, b, (((1,), (1,)), ((), ())), preferred_element_type=f32)


def start_copies(sources, targets, sems):
    copies = [
        pltpu.make_async_copy(source, target, sems.at[i])
        for i, (source, target) in enumerate(zip(sources, targets))
    ]
    for copy in copies:
        copy.start()
    return copies


def like(arrays):
    return [pltpu.VMEM(a.shape, a.dtype) for a in arrays]


def silu(v):
    return v / (1.0 + jnp.exp(-v))


def position_table(token_count, width):
    half = width // 2
    rates = np.exp(-math.log(10000.0) * np.arange(half) / half)
    angles = np.arange(token_count)[:, None] * rates[None, :]
    return np.concatenate([np.sin(angles), np.cos(angles)], axis=1).astype(np.float32)


def tell_kernel(time_hbm, step_hbm, labels_hbm, out_ref, time_ref, step_ref, labels_ref, block, sems):
    copies = start_copies(
        (time_hbm, step_hbm, labels_hbm), (time_ref, step_ref, labels_ref), sems
    )
    block[...] = jnp.zeros_like(block)
    for copy in copies:
        copy.wait()
    mine = lax.axis_index("tensor")
    tiles = labels_ref.shape[1] // LANES
    both = labels_ref[...].astype(f32)
    row = jnp.where(mine == 0, both[0:1], both[1:2])
    for tile in range(tiles):
        block[tile : tile + 1, :] = row[:, tile * LANES : (tile + 1) * LANES]
    now = time_ref[mine]
    later = now - step_ref[mine]
    block[tiles : tiles + 1, :] = jnp.full((1, LANES), now, f32)
    block[tiles + 1 : tiles + 2, :] = jnp.full((1, LANES), later, f32)
    for dest in range(out_ref.shape[0]):
        out_ref[dest] = block[...]


def part_kernel(heard_ref, *refs):
    sources, out_ref, sems = refs[:10], refs[10], refs[-1]
    time_in_ref, time_out_ref, ada_near, ada_far, fin_near, fin_far, part = refs[11:18]
    own_rows = sources[2].shape[0]
    second = up(own_rows, SUB)
    stacks = (ada_near, ada_far, fin_near, fin_far)
    stages = refs[18:-1]
    copies = [
        pltpu.make_async_copy(sources[0], time_in_ref, sems.at[0]),
        pltpu.make_async_copy(sources[1], time_out_ref, sems.at[1]),
    ]
    for at, source in enumerate(sources[2:]):
        stack = stacks[at // 2]
        first = at % 2 * second
        target = stages[at] if stages else stack.at[pl.ds(first, own_rows), :]
        copies.append(pltpu.make_async_copy(source, target, sems.at[2 + at]))
    for copy in copies[:2]:
        copy.start()
    count = heard_ref.shape[0]
    width = time_out_ref.shape[0]
    tiles = width // LANES
    labels = jnp.concatenate([heard_ref[:, tile, :] for tile in range(tiles)], axis=1)
    labels = jnp.concatenate([labels, labels], axis=0)
    moments = jnp.concatenate([heard_ref[:, tiles, :], heard_ref[:, tiles + 1, :]], axis=0)
    half_freq = time_in_ref.shape[0] // 2
    index = lax.broadcasted_iota(jnp.int32, (1, half_freq), 1).astype(f32)
    rates = jnp.exp(index * (-math.log(10000.0) / half_freq))
    angles = 1000.0 * moments * rates
    features = jnp.concatenate([jnp.cos(angles), jnp.sin(angles)], axis=1).astype(bf16)
    place = lax.axis_index("dp")
    pair = place + 1 - 2 * lax.rem(place, 2)
    depth = ada_near.shape[0]
    pick_shape = (width, depth)
    at_row = lax.broadcasted_iota(jnp.int32, pick_shape, 0)
    at_lane = lax.broadcasted_iota(jnp.int32, pick_shape, 1)
    mine = (at_lane < own_rows) & (at_row == at_lane + place * own_rows)
    theirs = (at_lane >= second) & (at_lane < second + own_rows)
    theirs = theirs & (at_row == at_lane - second + pair * own_rows)
    pick = jnp.where(mine | theirs, 1.0, 0.0).astype(bf16)
    copies[0].wait()
    for copy in copies[2:]:
        copy.start()
    hidden = silu(mm(features, time_in_ref[...])).astype(bf16)
    copies[1].wait()
    cond = silu(labels + mm(hidden, time_out_ref[...])).astype(bf16)
    own_cond = mm(cond, pick).astype(bf16)
    low = lax.axis_index("tensor") == 0
    for copy in copies[2:]:
        copy.wait()
    for at, stage in enumerate(stages):
        first = at % 2 * second
        stacks[at // 2][first : first + own_rows, :] = stage[...]
    if second != own_rows:
        for stack in stacks:
            for first in (own_rows, second + own_rows):
                stack[first : first + second - own_rows, :] = jnp.zeros(
                    (second - own_rows, stack.shape[1]), bf16
                )
    wide = up(ada_near.shape[1], LANES)
    for at, near, far in ((0, ada_near, ada_far), (2 * wide, fin_near, fin_far)):
        a = mm(own_cond, near[...])
        b = mm(own_cond, far[...])
        used = a.shape[1]
        gap = up(used, LANES)
        part[:, at : at + used] = jnp.where(low, a, b)
        part[:, at + gap : at + gap + used] = jnp.where(low, b, a)
        if gap != used:
            part[:, at + used : at + gap] = jnp.zeros((2 * count, gap - used), f32)
            part[:, at + gap + used : at + 2 * gap] = jnp.zeros((2 * count, gap - used), f32)
    for dest in range(count):
        now_row = part[dest : dest + 1, :]
        later_row = part[count + dest : count + dest + 1, :]
        out_ref[dest] = jnp.concatenate([now_row, later_row], axis=0).astype(bf16)


def norm(v):
    width = v.shape[1]
    average = jnp.sum(v, axis=1, keepdims=True) * (1.0 / width)
    centred = v - average
    spread_sq = jnp.sum(centred * centred, axis=1, keepdims=True) * (1.0 / width)
    return centred * lax.rsqrt(spread_sq + norm_eps)


def step_kernel(
    time_hbm, step_hbm, accept_hbm, mods_ref, *refs,
):
    sources, out_ref, rest_refs = refs[:9], refs[9], refs[18:]
    cur_ref, noise_ref, patch_ref, pos_ref, qkv_own, qkv_other, out_all, proj_ref = refs[10:18]
    half = qkv_own.shape[1]
    targets = (
        cur_ref, noise_ref, patch_ref, pos_ref, qkv_own, qkv_other,
        out_all.at[pl.ds(0, half), :], out_all.at[pl.ds(half, half), :], proj_ref,
    )
    time_ref, step_ref, accept_ref, sems, *work = rest_refs
    early = start_copies(
        (time_hbm, step_hbm, accept_hbm), (time_ref, step_ref, accept_ref), sems.at[pl.ds(9, 3)]
    )
    copies = [pltpu.make_async_copy(s, t, sems.at[i]) for i, (s, t) in enumerate(zip(sources, targets))]
    for at in (0, 1, 2, 8, 3, 4, 5, 6, 7):
        copies[at].start()
    for copy in early + copies[:3] + copies[8:]:
        copy.wait()
    step_body(
        time_ref, step_ref, accept_ref, cur_ref, noise_ref, pos_ref, patch_ref,
        qkv_own, qkv_other, out_all, proj_ref, mods_ref, out_ref, copies[3:8], *work,
    )


def step_body(
    time_ref, step_ref, accept_ref, cur_ref, noise_ref, pos_ref, patch_ref,
    qkv_own, qkv_other, out_all, proj_ref, mods_ref, out_ref, copies,
    cur32, nse32, state32, guess32, modv, patch8, proj8, stream, inner, query, keys, value, mixed,
    scores, probs, turned,
):
    mine = lax.axis_index("tensor")
    low_core = mine == 0
    lat_rows = cur32.shape[0]
    tokens, width = stream.shape
    half = qkv_own.shape[1]
    heads = half // HEAD_DIM
    count = mods_ref.shape[0]
    vals = patch_ref.shape[0]
    reps = LANES // vals

    for row in range(lat_rows):
        lanes = slice(row * LANES, (row + 1) * LANES)
        cur32[row : row + 1, :] = jnp.where(low_core, cur_ref[0:1, lanes], cur_ref[1:2, lanes])
        nse32[row : row + 1, :] = jnp.where(low_core, noise_ref[0:1, lanes], noise_ref[1:2, lanes])
    for rep in range(reps):
        patch8[rep * vals : (rep + 1) * vals, :] = patch_ref[...]
        proj8[rep * vals : (rep + 1) * vals, :] = proj_ref[...]
    query[:, half:, :] = jnp.zeros((2, query.shape[1] - half, tokens), bf16)
    keys[:, :, half:] = jnp.zeros((2, tokens, keys.shape[2] - half), bf16)

    total = mods_ref[0].astype(f32)
    for source in range(1, count):
        total = total + mods_ref[source].astype(f32)
    lay_cols = 3 * width // 2
    wide = up(lay_cols, LANES)
    low = total[:, :wide]
    high = total[:, wide : 2 * wide]
    lane = lax.broadcasted_iota(jnp.int32, (2, width), 1)
    rest = low[:, width:]
    rest = jnp.concatenate([rest, jnp.zeros((2, width - rest.shape[1]), f32)], axis=1)
    split = lay_cols - width
    scale_attn = jnp.where(lane < split, rest, pltpu.roll(high[:, :width], split, 1))
    gate_attn = pltpu.roll(high, wide - (width - split), 1)[:, :width]
    for moment in range(2):
        row = slice(moment, moment + 1)
        modv[moment, 0:1, :] = low[row, :width]
        modv[moment, 1:2, :] = 1.0 + scale_attn[row]
        modv[moment, 2:3, :] = gate_attn[row]
        modv[moment, 3:4, :] = total[row, 2 * wide : 2 * wide + width]
        modv[moment, 4:5, :] = 1.0 + total[row, 2 * wide + width : 2 * wide + 2 * width]

    now = jnp.full((1, LANES), time_ref[mine], f32)
    step = jnp.full((1, LANES), step_ref[mine], f32)
    later = now - step

    def beta_at(m):
        return beta_low + (beta_high - beta_low) * m

    def drift(values, m, guess):
        rate = beta_at(m)
        integral = beta_low * m + 0.5 * (beta_high - beta_low) * m * m
        return 0.5 * rate * values - rate * guess / jnp.sqrt(1.0 - jnp.exp(-integral))

    spread = jnp.sqrt(step * beta_at(now)) * nse32[...]
    group = lax.broadcasted_iota(jnp.int32, (tokens, LANES), 1) // vals
    own_slot = group == lax.broadcasted_iota(jnp.int32, (tokens, LANES), 0) % reps
    exp_scale = HEAD_DIM**-0.5 * math.log2(math.e)

    def fetched(index, which):
        @pl.when(index == 0)
        def _():
            copies[which].wait()

    ones = jnp.ones((ROWS, tokens), f32)

    def project(part, kind, weight):
        raw = mm_t(weight[kind], inner[...])
        if kind == 0:
            query[part, :half, :] = raw.astype(bf16)
        elif kind == 1:
            keys[part, :, :half] = raw.astype(bf16).T
        else:
            for head in range(heads):
                rows = slice(head * HEAD_DIM, (head + 1) * HEAD_DIM)
                value[part, head] = jnp.concatenate([raw[rows], ones], axis=0).astype(bf16)

    def score(at):
        part, head = divmod(at, heads)
        begin = head * HEAD_DIM
        lo = begin // LANES * LANES
        hi = up(begin + HEAD_DIM, LANES)
        row = lax.broadcasted_iota(jnp.int32, (hi - lo, tokens), 0) + lo
        inside = (row >= begin) & (row < begin + HEAD_DIM)
        q = jnp.where(inside, query[part, lo:hi, :], jnp.zeros((), bf16))
        scores[at % SLOTS] = mm(keys[part, :, lo:hi], q)

    def evaluate(index, carry):
        del carry
        x = state32[...]
        tok = jnp.broadcast_to(x[:, None, :], (lat_rows, reps, LANES)).reshape(tokens, LANES)
        tok = jnp.where(own_slot, tok, 0.0).astype(bf16)
        fetched(index, 0)
        stream[...] = mm(tok, patch8[...]) + pos_ref[...]
        inner[...] = (norm(stream[...]) * modv[index, 1:2, :] + modv[index, 0:1, :]).astype(bf16)
        fetched(index, 1)
        fetched(index, 2)
        fetched(index, 3)
        fetched(index, 4)
        for kind in range(3):
            project(0, kind, qkv_own)
        for at in range(AHEAD):
            score(at)
        got = {}
        for at in range(2 * heads):
            if at < 3:
                project(1, (1, 0, 2)[at], qkv_other)
            raw = scores[at % SLOTS]
            top = jnp.max(raw, axis=0, keepdims=True)
            probs[at % 2] = jnp.exp2((raw - top) * exp_scale).astype(bf16)
            if at + AHEAD < 2 * heads:
                score(at + AHEAD)
            part, head = divmod(at, heads)
            mix = mm(value[part, head], probs[at % 2])
            got[at] = mix[:HEAD_DIM] * (1.0 / mix[HEAD_DIM : HEAD_DIM + 1])
            if at % 2:
                pair = jnp.concatenate([got.pop(at - 1), got.pop(at)], axis=0)
                first = (at - 1) * HEAD_DIM
                mixed[first : first + 2 * HEAD_DIM, :] = pair.astype(bf16)
        turned[...] = mixed[...].T
        stream[...] += modv[index, 2:3, :] * mm(turned[...], out_all[...])
        inner[...] = (norm(stream[...]) * modv[index, 4:5, :] + modv[index, 3:4, :]).astype(bf16)
        guess = jnp.where(own_slot, mm_t(inner[...], proj8[...]), 0.0)
        guess = jnp.sum(guess.reshape(lat_rows, reps, LANES), axis=1)
        guess32[index] = guess

        @pl.when(index == 0)
        def _():
            state32[...] = cur32[...] + step * drift(cur32[...], now, guess) + spread

        return 0

    state32[...] = cur32[...]
    lax.fori_loop(0, 2, evaluate, 0)

    cur = cur32[...]
    euler = state32[...]
    drift_now = drift(cur, now, guess32[0])
    drift_later = drift(euler, later, guess32[1])
    heun = cur + 0.5 * step * (drift_now + drift_later) + spread
    scale_ref = jnp.maximum(tol_abs, tol_rel * jnp.maximum(jnp.abs(heun), jnp.abs(cur)))
    gap = (euler - heun) / scale_ref
    square = jnp.sum(jnp.sum(gap * gap, axis=1, keepdims=True), axis=0, keepdims=True)
    error = jnp.sqrt(square / (lat_rows * LANES))
    out_ref[:lat_rows, :] = jnp.where(accept_ref[mine] == 1, heun, cur)
    out_ref[lat_rows:, :] = jnp.broadcast_to(error, (ROWS, LANES))


def join_kernel(done_ref, other_ref, state_ref, error_ref):
    low = lax.axis_index("tensor") == 0
    lat_rows = state_ref.shape[1] // LANES
    done, other = done_ref[...], other_ref[...]
    first, second = jnp.where(low, done, other), jnp.where(low, other, done)
    for row in range(lat_rows):
        lanes = slice(row * LANES, (row + 1) * LANES)
        state_ref[0:1, lanes] = first[row : row + 1]
        state_ref[1:2, lanes] = second[row : row + 1]
    error_ref[0] = jnp.max(first[lat_rows:])
    error_ref[1] = jnp.max(second[lat_rows:])


def shards(
    current, noise_draw, labels, time_now, step_size, accept, patch_weight, time_in,
    time_out, qkv_weight, out_weight, ada_weight, final_ada, final_proj,
):
    members = lax.axis_size("dp")
    count = members // 2
    groups = [[2 * i + side for i in range(count)] for side in range(2)]
    trade = functools.partial(
        lax.ppermute, axis_name="dp", perm=[(i, i ^ 1) for i in range(members)]
    )
    width = time_out.shape[0]
    latent = current.shape[1]
    vals = patch_weight.shape[0]
    tokens = latent // vals
    half = qkv_weight.shape[3]
    swap = functools.partial(lax.ppermute, axis_name="tensor", perm=[(0, 1), (1, 0)])

    qkv = qkv_weight[0].transpose(1, 2, 0)
    out = out_weight[0].T
    ada = ada_weight[0]

    ada_pair, fin_pair = trade(ada), trade(final_ada)
    ada_other, fin_other = swap(ada), swap(final_ada)
    qkv_other, out_other = swap(qkv), swap(out)

    tell_rows = up(width // LANES + 2, ROWS)
    told = pl.pallas_call(
        tell_kernel,
        out_shape=jax.ShapeDtypeStruct((count, tell_rows, LANES), f32),
        in_specs=[HBM, HBM, HBM],
        out_specs=VM,
        scratch_shapes=[
            pltpu.SMEM(time_now.shape, f32),
            pltpu.SMEM(step_size.shape, f32),
            pltpu.VMEM(labels.shape, labels.dtype),
            pltpu.VMEM((tell_rows, LANES), f32),
            pltpu.SemaphoreType.DMA((3,)),
        ],
        compiler_params=pltpu.CompilerParams(vmem_limit_bytes=GRANT),
    )(time_now, step_size, labels)
    heard = lax.all_to_all(told, "dp", 0, 0, axis_index_groups=groups, tiled=True)
    heard, ada_pair, fin_pair = lax.optimization_barrier((heard, ada_pair, fin_pair))
    ada_pair_other, fin_pair_other = swap(ada_pair), swap(fin_pair)

    cols = 2 * up(ada.shape[1], LANES) + 2 * final_ada.shape[1]
    depth = 2 * up(ada.shape[0], SUB)
    near = (
        time_in, time_out, ada, ada_pair, ada_other, ada_pair_other,
        final_ada, fin_pair, fin_other, fin_pair_other,
    )
    parts = pl.pallas_call(
        part_kernel,
        out_shape=jax.ShapeDtypeStruct((count, 2, cols), bf16),
        in_specs=[VM] + [HBM] * len(near),
        out_specs=VM,
        scratch_shapes=like(near[:2])
        + [pltpu.VMEM((depth, a.shape[1]), bf16) for a in (ada, ada, final_ada, final_ada)]
        + [pltpu.VMEM((2 * count, cols), f32)]
        + (like(near[2:]) if ada.shape[0] % ROWS else [])
        + [pltpu.SemaphoreType.DMA((len(near),))],
        compiler_params=pltpu.CompilerParams(vmem_limit_bytes=GRANT_ALL),
    )(heard, *near)
    mods = lax.all_to_all(parts, "dp", 0, 0, axis_index_groups=groups, tiled=True)

    lat_rows = latent // LANES
    padded = up(half, LANES)
    positions = jnp.asarray(position_table(tokens, width))
    small = pltpu.VMEM((lat_rows, LANES), f32)
    held = (
        current, noise_draw, patch_weight, positions, qkv, qkv_other, out, out_other, final_proj.T
    )
    done = pl.pallas_call(
        step_kernel,
        out_shape=jax.ShapeDtypeStruct((lat_rows + ROWS, LANES), f32),
        in_specs=[HBM, HBM, HBM, VM] + [HBM] * len(held),
        out_specs=VM,
        scratch_shapes=like(held[:6])
        + [pltpu.VMEM((width, width), bf16)]
        + like(held[8:])
        + [
            pltpu.SMEM(time_now.shape, f32),
            pltpu.SMEM(step_size.shape, f32),
            pltpu.SMEM(accept.shape, accept.dtype),
            pltpu.SemaphoreType.DMA((len(held) + 3,)),
            small, small, small,
            pltpu.VMEM((2, lat_rows, LANES), f32),
            pltpu.VMEM((2, ROWS, width), f32),
            pltpu.VMEM((LANES, width), bf16),
            pltpu.VMEM((LANES, width), bf16),
            pltpu.VMEM((tokens, width), f32),
            pltpu.VMEM((tokens, width), bf16),
            pltpu.VMEM((2, padded, tokens), bf16),
            pltpu.VMEM((2, tokens, padded), bf16),
            pltpu.VMEM((2, half // HEAD_DIM, HEAD_DIM + ROWS, tokens), bf16),
            pltpu.VMEM((2 * half, tokens), bf16),
            pltpu.VMEM((SLOTS, tokens, tokens), f32),
            pltpu.VMEM((2, tokens, tokens), bf16),
            pltpu.VMEM((tokens, 2 * half), bf16),
        ],
        compiler_params=pltpu.CompilerParams(vmem_limit_bytes=GRANT),
    )(
        time_now, step_size, accept, mods, *held,
    )
    other = swap(done)
    return pl.pallas_call(
        join_kernel,
        out_shape=(
            jax.ShapeDtypeStruct((2, latent), f32),
            jax.ShapeDtypeStruct((2,), f32),
        ),
        in_specs=[VM, VM],
        out_specs=(VM, SM),
        compiler_params=pltpu.CompilerParams(vmem_limit_bytes=GRANT_ALL),
    )(done, other)


def solution(mesh):
    in_specs = (
        P("dp", None),
        P("dp", None),
        P("dp", None),
        P("dp"),
        P("dp"),
        P("dp"),
        P(),
        P(),
        P(),
        P(None, None, None, "tensor"),
        P(None, None, "tensor"),
        P(None, "dp", "tensor"),
        P("dp", "tensor"),
        P(),
    )
    out_specs = (P("dp", None), P("dp"))
    return jax.shard_map(shards, mesh=mesh, in_specs=in_specs, out_specs=out_specs, check_vma=False)
```
